128 devices in a mesh: walk: 16 (over x, y_lo, core), chol: 8 (over z, y_hi).
Axes of the slice: x: 4, y: 4 (y_hi: 2, y_lo: 2; y = y_hi * 2 + y_lo), z: 4, core: 2. Of those that a mesh axis runs over, the one named last changes fastest.
Arguments:
- orbitals: float32 [256, 32, 512], P(('walk', 'chol')), may hold values from -3 to 3
- dest: int32 [256, 2], P(('walk', 'chol')), may hold values from -1 to 15, as said below
- chol_vectors: bfloat16 [2048, 32, 512], P('chol'), may hold values from -2 to 2
Outputs:
- energy: float32 [512], P(('walk', 'chol'))
- force_bias: float32 [512, 2048], P(('walk', 'chol'))
- log_correlation: float32 [512], P(('walk', 'chol'))
The draws below stay inside these ranges and needn't reach their ends.
Inputs may be any that keep to these rules, and one draw needn't show every extreme that they name: `dest`: entry (r, k) names the walk index that receives copy k of walker r, or -1 where that copy is not made. Among the devices that share a chol index, each device sends exactly 2 copies, at most one of them to any walk index; half of the walk indices receive exactly 4 copies and the others none.
All inputs are finite; a program needn't handle non-finite values.
Results may differ from the reference program's by a relative error of at most 0.0029.
Values may be sent and summed in bfloat16 or wider, within the bound.
No kernel may reach another device: no remote copies, remote signals or barrier semaphores. Data moves between devices by JAX's collectives and lax.ppermute only.
A program may use at most 128 MiB of HBM per device.

```python
import math
import jax
import jax.numpy as jnp
from jax import lax

BASIS = 512
ELEC = 32
CHOL_DEV = 256
WALK_DEV = 2
RECV = 4
NCHOL = 2048
OLD_WALKERS = 256
NEW_SLOTS = 512
N_WALK = 16
N_CHOL = 8


def draw_orbitals(key, part):
    first, second = jax.random.split(key, 2)
    noise = jnp.clip(jax.random.normal(first, (OLD_WALKERS, ELEC, ELEC), jnp.float32), -6.0, 6.0)
    tail = 0.5 * jnp.clip(jax.random.normal(second, (OLD_WALKERS, ELEC, BASIS - ELEC), jnp.float32), -6.0, 6.0)
    head = 1.5 * jnp.eye(ELEC, dtype=jnp.float32)[None] + 0.06 * noise
    return jnp.concatenate([head, tail], axis=2)


def draw_chol_vectors(key, part):
    first, second = jax.random.split(key, 2)
    ramp = 1.0 + 2.0 * jnp.arange(NCHOL, dtype=jnp.float32) / max(NCHOL - 1, 1)
    jitter = jnp.exp(jax.random.uniform(first, (NCHOL,), jnp.float32, -0.22, 0.22))
    values = jnp.clip(jax.random.normal(second, (NCHOL, ELEC, BASIS), jnp.float32), -4.0, 4.0)
    scaled = values * (ramp * jitter)[:, None, None] / math.sqrt(BASIS)
    return scaled.astype(jnp.bfloat16)


def draw_dest(key, part):
    half = N_WALK // 2
    copies = 2 * WALK_DEV
    first, second, third = jax.random.split(key, 3)
    hot = jax.vmap(lambda item: jax.random.permutation(item, N_WALK))(jax.random.split(first, N_CHOL)).astype(jnp.int32)
    order = jax.vmap(lambda item: jax.random.permutation(item, N_WALK))(jax.random.split(second, N_CHOL)).astype(jnp.int32)
    places = jax.vmap(lambda item: jax.random.permutation(item, copies))(jax.random.split(third, N_CHOL * N_WALK))
    places = places.astype(jnp.int32).reshape(N_CHOL, N_WALK, copies)
    offset = jnp.arange(WALK_DEV, dtype=jnp.int32)
    position = (order[:, :, None] + offset[None, None, :]) % half
    target = jnp.take_along_axis(hot, position.reshape(N_CHOL, N_WALK * WALK_DEV), axis=1)
    target = target.reshape(N_CHOL, N_WALK, WALK_DEV)
    onehot = places[:, :, :WALK_DEV, None] == jnp.arange(copies, dtype=jnp.int32)[None, None, None, :]
    table = jnp.sum(jnp.where(onehot, target[..., None] + 1, 0), axis=2) - 1
    return table.transpose(1, 0, 2).reshape(OLD_WALKERS, 2).astype(jnp.int32)


def setup_inputs(seed: int = 0) -> dict:
    splits = jax.random.split(jax.random.key(seed), 4)
    return {
        "orbitals": draw_orbitals(jax.random.fold_in(splits[3], 71), 0),
        "dest": draw_dest(jax.random.fold_in(splits[3], 71), 0),
        "chol_vectors": draw_chol_vectors(jax.random.fold_in(splits[3], 71), 0),
    }


def correlation_green(walkers):
    elec = walkers.shape[1]
    square = walkers[:, :, :elec]
    gram = jnp.einsum('wba,wbc->wac', square, square, precision=lax.Precision.HIGHEST)
    rotated = jnp.einsum('wba,wbm->wam', square, walkers, precision=lax.Precision.HIGHEST)
    factor = jnp.linalg.cholesky(gram)
    middle = lax.linalg.triangular_solve(factor, rotated, left_side=True, lower=True)
    green = lax.linalg.triangular_solve(factor, middle, left_side=True, lower=True, transpose_a=True)
    diagonal = jnp.diagonal(factor, axis1=1, axis2=2)
    log_correlation = jnp.sum(jnp.log(diagonal), axis=1) / elec
    return (green.astype(jnp.bfloat16), log_correlation)

def stop_terms(vectors, block):
    count, elec, basis = vectors.shape
    walkers = block.shape[0]
    product = jnp.dot(vectors.reshape(count * elec, basis).astype(jnp.float32), block.reshape(walkers * elec, basis).T.astype(jnp.float32), preferred_element_type=jnp.float32).reshape(count, elec, walkers, elec)
    values = jnp.einsum('giwj,ij->wg', product, jnp.eye(elec, dtype=jnp.float32))
    crossed = jnp.einsum('giwj,gjwi->wg', product, product)
    return (values, crossed)

def reference(orbitals, dest, chol_vectors):
    entries = dest.reshape(-1)
    entry_ids = jnp.arange(entries.shape[0], dtype=jnp.int32)
    rows = entry_ids // 2
    group = rows // WALK_DEV % N_CHOL
    alive = entries >= 0
    target = entries * N_CHOL + group
    same = (target[:, None] == target[None, :]) & alive[None, :] & (entry_ids[None, :] < entry_ids[:, None])
    rank = jnp.sum(same.astype(jnp.int32), axis=1).astype(jnp.int32)
    slot = jnp.where(alive, target * RECV + rank, NEW_SLOTS).astype(jnp.int32)
    trial = jnp.eye(ELEC, BASIS, dtype=jnp.float32)
    walkers = jnp.broadcast_to(trial, (NEW_SLOTS, ELEC, BASIS))
    walkers = walkers.at[slot].set(orbitals[rows], mode='drop')
    filled = jnp.zeros((NEW_SLOTS,), jnp.float32).at[slot].set(1.0, mode='drop')
    green, log_correlation = correlation_green(walkers)
    blocks = green.reshape(N_WALK, RECV * N_CHOL, ELEC, BASIS)
    vector_blocks = chol_vectors.reshape(N_CHOL, CHOL_DEV, ELEC, BASIS)

    def per_row(block):

        def per_chol(vectors):
            return stop_terms(vectors, block)
        values, crossed = lax.map(per_chol, vector_blocks)
        values = values.transpose(1, 0, 2).reshape(RECV * N_CHOL, NCHOL)
        crossed = crossed.transpose(1, 0, 2).reshape(RECV * N_CHOL, NCHOL)
        energy = jnp.sum(2.0 * values * values - crossed, axis=1) / (ELEC * NCHOL)
        return (values, energy)
    bias, energy = lax.map(per_row, blocks)
    bias = bias.reshape(NEW_SLOTS, NCHOL)
    energy = energy.reshape(NEW_SLOTS)
    return (energy * filled, bias * filled[:, None], log_correlation * filled)
```

```python
import functools

import jax
import jax.numpy as jnp
from jax import lax
from jax.experimental import pallas as pl
from jax.experimental.pallas import tpu as pltpu
from jax.sharding import PartitionSpec as P

F32 = jnp.float32
BF16 = jnp.bfloat16
HIGH = lax.Precision.HIGHEST


def iota(shape, axis):
    return lax.broadcasted_iota(jnp.int32, shape, axis)


def green_kernel(dest_ref, walkers_ref, packet_ref, log_ref):
    count, elec, basis = walkers_ref.shape
    work = []
    for r in range(count):
        full = walkers_ref[r]
        work.append(
            lax.dot_general(
                full[:, :elec], full, (((0,), (0,)), ((), ())), precision=HIGH, preferred_element_type=F32
            )
        )
    rows = iota((elec, 1), 0)
    lanes = iota((8, 128), 1)
    pivots = [jnp.ones((1, 128), F32) for _ in range(count)]
    lane = iota((1, 128), 1)
    for k in range(elec):
        for r in range(count):
            a = work[r]
            row = a[k : k + 1, :]
            column = a[:, k : k + 1]
            pivot = row[:, k : k + 1]
            inverse = 1.0 / pivot
            pivots[r] = jnp.where(lane == k, pivot, pivots[r])
            scaled = row * inverse
            work[r] = jnp.where(rows == k, scaled, a - column * scaled)
    out = jnp.zeros((8, 128), F32)
    for r in range(count):
        wanted = (dest_ref[r, 0] >= 0) | (dest_ref[r, 1] >= 0)
        packet_ref[r * elec : (r + 1) * elec, :] = jnp.where(wanted, work[r], 0.0).astype(BF16)
        total = jnp.sum(jnp.where(lane < elec, jnp.log(pivots[r]), 0.0), axis=1, keepdims=True)
        total = jnp.where(wanted, total * (0.5 / elec), 0.0)
        out = jnp.where(lanes == r, total, out)
    log_ref[...] = out
    tag = jnp.full((8, basis), -1.0, F32)
    wide = iota((8, basis), 1)
    for r in range(count):
        for k in range(2):
            tag = jnp.where(wide == 2 * r + k, dest_ref[r, k].astype(F32), tag)
    packet_ref[count * elec :, :] = tag.astype(BF16)


def green_of(orbitals, dest):
    count, elec, basis = orbitals.shape
    rows = count * elec + 8
    return pl.pallas_call(
        green_kernel,
        out_shape=(jax.ShapeDtypeStruct((rows, basis), BF16), jax.ShapeDtypeStruct((8, 128), F32)),
        in_specs=[pl.BlockSpec(memory_space=pltpu.SMEM), pl.BlockSpec(memory_space=pltpu.VMEM)],
        out_specs=(pl.BlockSpec(memory_space=pltpu.VMEM), pl.BlockSpec(memory_space=pltpu.VMEM)),
        cost_estimate=pl.CostEstimate(flops=8_000_000, bytes_accessed=200_000, transcendentals=64),
        name="green",
    )(dest, orbitals)


def relayout_kernel(vectors_ref, out_ref):
    elec, group, basis = out_ref.shape
    half = group // 2
    size = half * elec
    to = iota((size, size), 0)
    of = iota((size, size), 1)
    move = ((to % half) * elec + to // half == of).astype(BF16)
    parts = []
    for h in range(2):
        moved = jnp.dot(move, vectors_ref[h * size : (h + 1) * size, :], preferred_element_type=F32)
        parts.append(moved.reshape(elec, half, basis))
    out_ref[...] = jnp.concatenate(parts, axis=1).astype(BF16)


def relayout(vectors):
    count, elec, basis = vectors.shape
    group = 16
    return pl.pallas_call(
        relayout_kernel,
        out_shape=jax.ShapeDtypeStruct((elec, count, basis), BF16),
        grid=(count // group,),
        in_specs=[pl.BlockSpec((group * elec, basis), lambda b: (b, 0))],
        out_specs=pl.BlockSpec((elec, group, basis), lambda b: (0, b, 0)),
        cost_estimate=pl.CostEstimate(
            flops=2 * count * elec * basis * 256, bytes_accessed=4 * count * elec * basis, transcendentals=0
        ),
        name="relayout",
    )(vectors.reshape(count * elec, basis))


def stop_kernel(me_ref, log_ref, *refs):
    block_refs, (vectors_ref, out_ref, green, kept, trace, cross) = refs[:4], refs[4:]
    step = pl.program_id(0)
    elec, _, walkers, count = kept.shape
    groups = 8
    per = walkers // groups
    chunk = vectors_ref.shape[0]
    basis = green.shape[1]
    me = me_ref[0]
    z, y = me // 2, me % 2

    @pl.when(step == 0)
    def _():
        size = walkers * elec
        stacked = jnp.concatenate(
            [ref[q, : per * elec, :] for ref in block_refs for q in range(2)], axis=0
        )
        to = iota((size, size), 0)
        of = iota((size, size), 1)
        j, r, c = to // walkers, (to // groups) % per, to % groups
        block = (((c // 2 + 4 - z) % 4) * 2) + ((c + y) % 2)
        move = ((block * per + r) * elec + j == of).astype(BF16)
        green[...] = jnp.dot(move, stacked, preferred_element_type=F32).astype(BF16)
        trace[...] = jnp.zeros_like(trace)
        cross[...] = jnp.zeros_like(cross)

    for ii in range(chunk):
        i = step * chunk + ii
        product = lax.dot_general(
            green[...], vectors_ref[ii], (((1,), (1,)), ((), ())), preferred_element_type=F32
        ).reshape(elec, walkers, count)
        total = jnp.zeros((walkers, count), F32)
        for j in range(elec):
            part = product[j]
            kept[j, i] = part
            total += jnp.where(j < i, part * kept[i, j], 0.0)
        same = kept[i, i]
        trace[...] += same
        cross[...] += total + 0.5 * (same * same)

    @pl.when(step == pl.num_programs(0) - 1)
    def _():
        lane = iota((groups, 128), 1)
        sub = iota((groups, 128), 0)
        tags = jnp.zeros((groups, 128), F32)
        for dz in range(4):
            for dy in range(2):
                tag = block_refs[dz][dy, per * elec :, :128].astype(F32)
                owner = ((z + dz) % 4) * 2 + (y + dy) % 2
                tags = jnp.where(sub == owner, tag, tags)
        values, wanted = [], []
        for r in range(per):
            bias = trace[r * groups : (r + 1) * groups, :]
            terms = 2.0 * (bias * bias) - 2.0 * cross[r * groups : (r + 1) * groups, :]
            energy = jnp.sum(terms, axis=1, keepdims=True)
            log = log_ref[:, r : r + 1]
            tail = jnp.where(lane == 0, 1.0, jnp.where(lane == 1, energy, 0.0))
            tail = jnp.where((lane == 2) & (sub == me), log, tail)
            values.append(jnp.concatenate([bias, tail], axis=1))
            wanted.append([tags[:, 2 * r + k : 2 * r + k + 1] for k in range(2)])
        for d in range(out_ref.shape[0] // groups):
            packet = jnp.zeros_like(values[0])
            for r in range(per):
                hit = (wanted[r][0] == float(d)) | (wanted[r][1] == float(d))
                packet = jnp.where(hit, values[r], packet)
            for c in range(groups):
                out_ref[d * groups + c] = packet[c : c + 1, :]


def stops(me, log, blocks, vectors, slots):
    elec, count, basis = vectors.shape
    walkers, chunk = 16, 4
    whole = pl.BlockSpec(memory_space=pltpu.VMEM)
    return pl.pallas_call(
        stop_kernel,
        out_shape=jax.ShapeDtypeStruct((slots, 1, count + 128), F32),
        grid=(elec // chunk,),
        in_specs=[pl.BlockSpec(memory_space=pltpu.SMEM), whole]
        + [whole] * len(blocks)
        + [pl.BlockSpec((chunk, count, basis), lambda b: (b, 0, 0))],
        out_specs=whole,
        scratch_shapes=[
            pltpu.VMEM((walkers * elec, basis), BF16),
            pltpu.VMEM((elec, elec, walkers, count), F32),
            pltpu.VMEM((walkers, count), F32),
            pltpu.VMEM((walkers, count), F32),
        ],
        cost_estimate=pl.CostEstimate(
            flops=2 * walkers * elec * elec * count * basis,
            bytes_accessed=2 * elec * count * basis,
            transcendentals=0,
        ),
        name="stops",
    )(me, log, *blocks, vectors)


def slot_kernel(scale, packets_ref, energy_ref, bias_ref, log_ref):
    slots, total = bias_ref.shape
    groups = 8
    width = packets_ref.shape[2]
    count = total // groups
    filled = jnp.zeros((groups, 1), F32)
    held = [jnp.zeros((groups, width), F32) for _ in range(slots)]
    for s in range(packets_ref.shape[0] // groups):
        packet = jnp.concatenate([packets_ref[s * groups + c] for c in range(groups)], axis=0)
        flag = packet[:, count : count + 1]
        for t in range(slots):
            held[t] = jnp.where((flag > 0.5) & (filled == float(t)), packet, held[t])
        filled = filled + flag
    for t in range(slots):
        for c in range(groups):
            bias_ref[t : t + 1, c * count : (c + 1) * count] = held[t][c : c + 1, :count]
        energy_ref[t] = jnp.sum(held[t][:, count + 1 : count + 2]) * scale
        log_ref[t] = jnp.sum(held[t][:, count + 2 : count + 3])


def slots_of(packets, slots, total, scale):
    return pl.pallas_call(
        functools.partial(slot_kernel, scale),
        out_shape=(
            jax.ShapeDtypeStruct((slots,), F32),
            jax.ShapeDtypeStruct((slots, total), F32),
            jax.ShapeDtypeStruct((slots,), F32),
        ),
        in_specs=[pl.BlockSpec(memory_space=pltpu.VMEM)],
        out_specs=(
            pl.BlockSpec(memory_space=pltpu.SMEM),
            pl.BlockSpec(memory_space=pltpu.VMEM),
            pl.BlockSpec(memory_space=pltpu.SMEM),
        ),
        name="slots",
    )(packets)


def moved(value, dz, dy):
    pairs = [
        (z * 2 + y, ((z + dz) % 4) * 2 + (y + dy) % 2) for z in range(4) for y in range(2)
    ]
    return lax.ppermute(value, "chol", pairs)


def body(orbitals, dest, chol_vectors):
    walk_count, chol_count = lax.axis_size("walk"), lax.axis_size("chol")
    walk_dev, elec, basis = orbitals.shape
    local = chol_vectors.shape[0]
    total = chol_count * local
    me = lax.axis_index("chol").astype(jnp.int32).reshape(1)
    packet, log = green_of(orbitals, dest)
    pair = jnp.stack([packet, moved(packet, 0, 1)])
    blocks = [pair, moved(pair, -1, 0), moved(pair, 2, 0), moved(pair, 1, 0)]
    vectors = relayout(chol_vectors)
    packets = stops(me, log, blocks, vectors, walk_count * chol_count)
    packets = lax.all_to_all(packets, ("walk", "chol"), split_axis=0, concat_axis=0, tiled=True)
    return slots_of(packets, 2 * walk_dev, total, 1.0 / (elec * total))


def solution(mesh):
    placed = (P(("walk", "chol"), None, None), P(("walk", "chol"), None), P("chol", None, None))
    return jax.shard_map(
        body,
        mesh=mesh,
        in_specs=placed,
        out_specs=(P(("walk", "chol")), P(("walk", "chol"), None), P(("walk", "chol"))),
        check_vma=False,
    )
```

```python
import functools

import jax
import jax.numpy as jnp
from jax import lax
from jax.experimental import pallas as pl
from jax.experimental.pallas import tpu as pltpu
from jax.sharding import PartitionSpec as P

F32 = jnp.float32
BF16 = jnp.bfloat16
MIB = 1 << 20
HIGH = lax.Precision.HIGHEST


def iota(shape, axis):
    return lax.broadcasted_iota(jnp.int32, shape, axis)


def prepare_kernel(
    places_ref, orbitals_ref, source_ref, packet_ref, log_ref, vectors_ref, dest_ref, walkers, held, landed, arrived
):
    count, elec, basis = walkers.shape
    total = held.shape[0]
    chunks = arrived.shape[0]
    size = total // chunks
    group = 16
    half = elec // 2

    def copy(n):
        part = pl.ds(n * size, size)
        return pltpu.make_async_copy(source_ref.at[part], held.at[part], arrived.at[n])

    fetch = pltpu.make_async_copy(orbitals_ref, walkers, landed.at[0])
    fetch.start()
    read = pltpu.make_async_copy(places_ref, dest_ref, landed.at[1])
    read.start()
    for n in range(chunks):
        copy(n).start()

    rows = group * half
    to = iota((rows, rows), 0)
    of = iota((rows, rows), 1)
    move = ((to % group) * half + to // group == of).astype(BF16)

    def relayout(n):
        g, h = n // 2, n % 2
        if n % (elec // chunks) == 0:
            copy(n // (elec // chunks)).wait()
        block = held[g * group : (g + 1) * group, h * half : (h + 1) * half, :].reshape(rows, basis)
        moved = jnp.dot(move, block, preferred_element_type=F32)
        vectors_ref[h * half : (h + 1) * half, g * group : (g + 1) * group, :] = moved.reshape(
            half, group, basis
        ).astype(BF16)

    fetch.wait()
    read.wait()
    work = []
    for r in range(count):
        full = walkers[r]
        work.append(
            lax.dot_general(
                full[:, :elec], full, (((0,), (0,)), ((), ())), precision=HIGH, preferred_element_type=F32
            )
        )
    sub = iota((elec, 1), 0)
    lane = iota((1, 128), 1)
    pivots = [jnp.ones((1, 128), F32) for _ in range(count)]
    for k in range(elec):
        for r in range(count):
            a = work[r]
            row = a[k : k + 1, :]
            column = a[:, k : k + 1]
            pivot = row[:, k : k + 1]
            pivots[r] = jnp.where(lane == k, pivot, pivots[r])
            scaled = row * (1.0 / pivot)
            work[r] = jnp.where(sub == k, scaled, a - column * scaled)
        relayout(k)
    out = jnp.zeros((8, 128), F32)
    lanes = iota((8, 128), 1)
    for r in range(count):
        wanted = (dest_ref[r, 0] >= 0) | (dest_ref[r, 1] >= 0)
        packet_ref[r * elec : (r + 1) * elec, :] = jnp.where(wanted, work[r], 0.0).astype(BF16)
        log = jnp.sum(jnp.where(lane < elec, jnp.log(pivots[r]), 0.0), axis=1, keepdims=True)
        log = jnp.where(wanted, log * (0.5 / elec), 0.0)
        out = jnp.where(lanes == r, log, out)
    log_ref[...] = out
    tag = jnp.full((8, basis), -1.0, F32)
    wide = iota((8, basis), 1)
    for r in range(count):
        for k in range(2):
            tag = jnp.where(wide == 2 * r + k, dest_ref[r, k].astype(F32), tag)
    packet_ref[count * elec :, :] = tag.astype(BF16)


def prepare(dest, orbitals, vectors):
    count, elec, basis = orbitals.shape
    total = vectors.shape[0]
    chunks = 8
    rows = count * elec + 8
    hbm = pl.BlockSpec(memory_space=pltpu.HBM)
    vmem = pl.BlockSpec(memory_space=pltpu.VMEM)
    return pl.pallas_call(
        prepare_kernel,
        out_shape=(
            jax.ShapeDtypeStruct((rows, basis), BF16),
            jax.ShapeDtypeStruct((8, 128), F32),
            jax.ShapeDtypeStruct((elec, total, basis), BF16),
        ),
        in_specs=[hbm, hbm, hbm],
        out_specs=(vmem, vmem, vmem),
        scratch_shapes=[
            pltpu.SMEM(dest.shape, jnp.int32),
            pltpu.VMEM(orbitals.shape, F32),
            pltpu.VMEM(vectors.shape, BF16),
            pltpu.SemaphoreType.DMA((2,)),
            pltpu.SemaphoreType.DMA((chunks,)),
        ],
        cost_estimate=pl.CostEstimate(
            flops=2 * total * elec * basis * 256, bytes_accessed=2 * total * elec * basis, transcendentals=64
        ),
        compiler_params=pltpu.CompilerParams(vmem_limit_bytes=20 * MIB),
        name="prepare",
    )(dest, orbitals, vectors)


def stop_kernel(log_ref, *refs):
    block_refs, vector_refs, (out_ref, green, kept) = refs[:5], refs[5:-3], refs[-3:]
    elec, _, walkers, count = kept.shape
    groups = 8
    per = walkers // groups
    basis = green.shape[1]
    me = lax.axis_index("chol")
    z, y = me // 2, me % 2
    packets = [block_refs[0][...], block_refs[1][...]]
    packets += [ref[q] for ref in block_refs[2:] for q in range(2)]

    size = walkers * elec
    stacked = jnp.concatenate([packet[: per * elec] for packet in packets], axis=0)
    to = iota((size, size), 0)
    of = iota((size, size), 1)
    j, r, c = to // walkers, (to // groups) % per, to % groups
    block = (((c // 2 + 4 - z) % 4) * 2) + ((c + y) % 2)
    move = ((block * per + r) * elec + j == of).astype(BF16)
    green[...] = jnp.dot(move, stacked, preferred_element_type=F32).astype(BF16)

    trace = jnp.zeros((walkers, count), F32)
    cross = jnp.zeros((walkers, count), F32)
    for i in range(elec):
        part = i
        for ref in vector_refs:
            if part < ref.shape[0]:
                vectors = ref[part]
                break
            part -= ref.shape[0]
        product = lax.dot_general(
            green[...], vectors, (((1,), (1,)), ((), ())), preferred_element_type=F32
        ).reshape(elec, walkers, count)
        for j in range(i + 1, elec):
            kept[j, i] = product[j]
        for j in range(i):
            cross = cross + product[j] * kept[i, j]
        trace = trace + product[i]
        cross = cross + 0.5 * (product[i] * product[i])

    lane = iota((groups, 128), 1)
    sub = iota((groups, 128), 0)
    tags = jnp.zeros((groups, 128), F32)
    for dz in range(4):
        for dy in range(2):
            tag = packets[dz * 2 + dy][per * elec :, :128].astype(F32)
            owner = ((z + dz) % 4) * 2 + (y + dy) % 2
            tags = jnp.where(sub == owner, tag, tags)
    values, wanted = [], []
    for r in range(per):
        bias = trace[r * groups : (r + 1) * groups, :]
        terms = 2.0 * (bias * bias) - 2.0 * cross[r * groups : (r + 1) * groups, :]
        energy = jnp.sum(terms, axis=1, keepdims=True)
        log = log_ref[:, r : r + 1]
        tail = jnp.where(lane == 0, 1.0, jnp.where(lane == 1, energy, 0.0))
        tail = jnp.where((lane == 2) & (sub == me), log, tail)
        values.append(jnp.concatenate([bias, tail], axis=1))
        wanted.append([tags[:, 2 * r + k : 2 * r + k + 1] for k in range(2)])
    for d in range(out_ref.shape[0] // groups):
        packet = jnp.zeros_like(values[0])
        for r in range(per):
            hit = (wanted[r][0] == float(d)) | (wanted[r][1] == float(d))
            packet = jnp.where(hit, values[r], packet)
        for c in range(groups):
            out_ref[d * groups + c] = packet[c : c + 1, :]


def stops(log, blocks, vectors, slots):
    elec = sum(part.shape[0] for part in vectors)
    _, count, basis = vectors[0].shape
    walkers = 16
    whole = pl.BlockSpec(memory_space=pltpu.VMEM)
    return pl.pallas_call(
        stop_kernel,
        out_shape=jax.ShapeDtypeStruct((slots, 1, count + 128), F32),
        in_specs=[whole] + [whole] * (len(blocks) + len(vectors)),
        out_specs=whole,
        scratch_shapes=[
            pltpu.VMEM((walkers * elec, basis), BF16),
            pltpu.VMEM((elec, elec, walkers, count), F32),
        ],
        cost_estimate=pl.CostEstimate(
            flops=2 * walkers * elec * elec * count * basis,
            bytes_accessed=2 * elec * count * basis,
            transcendentals=0,
        ),
        compiler_params=pltpu.CompilerParams(vmem_limit_bytes=30 * MIB),
        name="stops",
    )(log, *blocks, *vectors)


def slot_kernel(scale, packets_ref, energy_ref, bias_ref, log_ref):
    slots, total = bias_ref.shape
    groups = 8
    width = packets_ref.shape[2]
    count = total // groups
    filled = jnp.zeros((groups, 1), F32)
    held = [jnp.zeros((groups, width), F32) for _ in range(slots)]
    for s in range(packets_ref.shape[0] // groups):
        packet = jnp.concatenate([packets_ref[s * groups + c] for c in range(groups)], axis=0)
        flag = packet[:, count : count + 1]
        for t in range(slots):
            held[t] = jnp.where((flag > 0.5) & (filled == float(t)), packet, held[t])
        filled = filled + flag
    for t in range(slots):
        for c in range(groups):
            bias_ref[t : t + 1, c * count : (c + 1) * count] = held[t][c : c + 1, :count]
        energy_ref[t] = jnp.sum(held[t][:, count + 1 : count + 2]) * scale
        log_ref[t] = jnp.sum(held[t][:, count + 2 : count + 3])


def slots_of(packets, slots, total, scale):
    return pl.pallas_call(
        functools.partial(slot_kernel, scale),
        out_shape=(
            jax.ShapeDtypeStruct((slots,), F32),
            jax.ShapeDtypeStruct((slots, total), F32),
            jax.ShapeDtypeStruct((slots,), F32),
        ),
        in_specs=[pl.BlockSpec(memory_space=pltpu.VMEM)],
        out_specs=(
            pl.BlockSpec(memory_space=pltpu.SMEM),
            pl.BlockSpec(memory_space=pltpu.VMEM),
            pl.BlockSpec(memory_space=pltpu.SMEM),
        ),
        compiler_params=pltpu.CompilerParams(vmem_limit_bytes=4 * MIB),
        name="slots",
    )(packets)


def pair_kernel(first_ref, second_ref, out_ref):
    out_ref[0] = first_ref[...]
    out_ref[1] = second_ref[...]


def paired(first, second):
    return pl.pallas_call(
        pair_kernel,
        out_shape=jax.ShapeDtypeStruct((2,) + first.shape, first.dtype),
        in_specs=[pl.BlockSpec(memory_space=pltpu.VMEM)] * 2,
        out_specs=pl.BlockSpec(memory_space=pltpu.VMEM),
        compiler_params=pltpu.CompilerParams(vmem_limit_bytes=MIB),
        name="pair",
    )(first, second)


def moved(value, dz, dy):
    pairs = [
        (z * 2 + y, ((z + dz) % 4) * 2 + (y + dy) % 2) for z in range(4) for y in range(2)
    ]
    return lax.ppermute(value, "chol", pairs)


def body(orbitals, dest, chol_vectors):
    walk_count, chol_count = lax.axis_size("walk"), lax.axis_size("chol")
    walk_dev, elec, basis = orbitals.shape
    local = chol_vectors.shape[0]
    total = chol_count * local
    dest = pltpu.with_memory_space_constraint(dest, pltpu.HBM)
    orbitals = pltpu.with_memory_space_constraint(orbitals, pltpu.HBM)
    chol_vectors = pltpu.with_memory_space_constraint(chol_vectors, pltpu.HBM)
    packet, log, vectors = prepare(dest, orbitals, chol_vectors)
    other = moved(packet, 0, 1)
    pair = paired(packet, other)
    blocks = [packet, other, moved(pair, -1, 0), moved(pair, 2, 0), moved(pair, 1, 0)]
    packets = stops(log, blocks, [vectors], walk_count * chol_count)
    packets = lax.all_to_all(packets, ("walk", "chol"), split_axis=0, concat_axis=0, tiled=True)
    return slots_of(packets, 2 * walk_dev, total, 1.0 / (elec * total))


def solution(mesh):
    placed = (P(("walk", "chol"), None, None), P(("walk", "chol"), None), P("chol", None, None))
    return jax.shard_map(
        body,
        mesh=mesh,
        in_specs=placed,
        out_specs=(P(("walk", "chol")), P(("walk", "chol"), None), P(("walk", "chol"))),
        check_vma=False,
    )
```

```python
import functools

import jax
import jax.numpy as jnp
from jax import lax
from jax.experimental import pallas as pl
from jax.experimental.pallas import tpu as pltpu
from jax.sharding import PartitionSpec as P

F32 = jnp.float32
BF16 = jnp.bfloat16
MIB = 1 << 20
HIGH = lax.Precision.HIGHEST


def iota(shape, axis):
    return lax.broadcasted_iota(jnp.int32, shape, axis)


def green_kernel(places_ref, orbitals_ref, packet_ref, log_ref, dest_ref, walkers, landed):
    count, elec, basis = walkers.shape
    fetch = pltpu.make_async_copy(orbitals_ref, walkers, landed.at[0])
    fetch.start()
    read = pltpu.make_async_copy(places_ref, dest_ref, landed.at[1])
    read.start()
    fetch.wait()
    read.wait()
    work = []
    for r in range(count):
        full = walkers[r]
        work.append(
            lax.dot_general(
                full[:, :elec], full, (((0,), (0,)), ((), ())), precision=HIGH, preferred_element_type=F32
            )
        )
    sub = iota((elec, 1), 0)
    lane = iota((1, 128), 1)
    pivots = [jnp.ones((1, 128), F32) for _ in range(count)]
    for k in range(elec):
        for r in range(count):
            a = work[r]
            row = a[k : k + 1, :]
            column = a[:, k : k + 1]
            pivot = row[:, k : k + 1]
            pivots[r] = jnp.where(lane == k, pivot, pivots[r])
            scaled = row * (1.0 / pivot)
            work[r] = jnp.where(sub == k, scaled, a - column * scaled)
    out = jnp.zeros((8, 128), F32)
    lanes = iota((8, 128), 1)
    for r in range(count):
        wanted = (dest_ref[r, 0] >= 0) | (dest_ref[r, 1] >= 0)
        packet_ref[r * elec : (r + 1) * elec, :] = jnp.where(wanted, work[r], 0.0).astype(BF16)
        log = jnp.sum(jnp.where(lane < elec, jnp.log(pivots[r]), 0.0), axis=1, keepdims=True)
        log = jnp.where(wanted, log * (0.5 / elec), 0.0)
        out = jnp.where(lanes == r, log, out)
    log_ref[...] = out
    tag = jnp.full((8, basis), -1.0, F32)
    wide = iota((8, basis), 1)
    for r in range(count):
        for k in range(2):
            tag = jnp.where(wide == 2 * r + k, dest_ref[r, k].astype(F32), tag)
    packet_ref[count * elec :, :] = tag.astype(BF16)


def green_of(dest, orbitals):
    count, elec, basis = orbitals.shape
    rows = count * elec + 8
    hbm = pl.BlockSpec(memory_space=pltpu.HBM)
    vmem = pl.BlockSpec(memory_space=pltpu.VMEM)
    return pl.pallas_call(
        green_kernel,
        out_shape=(jax.ShapeDtypeStruct((rows, basis), BF16), jax.ShapeDtypeStruct((8, 128), F32)),
        in_specs=[hbm, hbm],
        out_specs=(vmem, vmem),
        scratch_shapes=[
            pltpu.SMEM(dest.shape, jnp.int32),
            pltpu.VMEM(orbitals.shape, F32),
            pltpu.SemaphoreType.DMA((2,)),
        ],
        cost_estimate=pl.CostEstimate(flops=8_000_000, bytes_accessed=200_000, transcendentals=64),
        compiler_params=pltpu.CompilerParams(vmem_limit_bytes=4 * MIB),
        name="green",
    )(dest, orbitals)


def relayout_kernel(first, vectors_ref, out_ref, held, arrived):
    elec, count, basis = out_ref.shape
    chunks = arrived.shape[0]
    size = count // chunks
    group = 16

    def copy(n):
        part = pl.ds(n * size, size)
        return pltpu.make_async_copy(
            vectors_ref.at[part, pl.ds(first, elec), :], held.at[part], arrived.at[n]
        )

    for n in range(chunks):
        copy(n).start()
    rows = group * elec
    to = iota((rows, rows), 0)
    of = iota((rows, rows), 1)
    move = ((to % group) * elec + to // group == of).astype(BF16)
    for n in range(chunks):
        copy(n).wait()
        for b in range(n * size // group, (n + 1) * size // group):
            block = held[b * group : (b + 1) * group].reshape(rows, basis)
            moved = jnp.dot(move, block, preferred_element_type=F32)
            out_ref[:, b * group : (b + 1) * group, :] = moved.reshape(elec, group, basis).astype(BF16)


def relayout(vectors, first, elec):
    count, _, basis = vectors.shape
    chunks = 8
    return pl.pallas_call(
        functools.partial(relayout_kernel, first),
        out_shape=jax.ShapeDtypeStruct((elec, count, basis), BF16),
        in_specs=[pl.BlockSpec(memory_space=pltpu.HBM)],
        out_specs=pl.BlockSpec(memory_space=pltpu.VMEM),
        scratch_shapes=[pltpu.VMEM((count, elec, basis), BF16), pltpu.SemaphoreType.DMA((chunks,))],
        cost_estimate=pl.CostEstimate(
            flops=2 * count * elec * basis * 256, bytes_accessed=2 * count * elec * basis, transcendentals=0
        ),
        compiler_params=pltpu.CompilerParams(vmem_limit_bytes=10 * MIB),
    )(vectors)


def sums_of(blocks, vector_refs, kept):
    elec, _, walkers, count = kept.shape
    per = walkers // len(blocks)
    size = walkers * elec
    stacked = jnp.concatenate([block[: per * elec] for block in blocks], axis=0)
    to = iota((size, size), 0)
    of = iota((size, size), 1)
    j, r, q = to // walkers, (to // len(blocks)) % per, to % len(blocks)
    move = ((q * per + r) * elec + j == of).astype(BF16)
    green = jnp.dot(move, stacked, preferred_element_type=F32).astype(BF16)
    trace = jnp.zeros((walkers, count), F32)
    cross = jnp.zeros((walkers, count), F32)
    for i in range(elec):
        ref = vector_refs[i * len(vector_refs) // elec]
        product = lax.dot_general(
            green, ref[i % ref.shape[0]], (((1,), (1,)), ((), ())), preferred_element_type=F32
        ).reshape(elec, walkers, count)
        for j in range(i + 1, elec):
            kept[j, i] = product[j]
        for j in range(i):
            cross = cross + product[j] * kept[i, j]
        trace = trace + product[i]
        cross = cross + 0.5 * (product[i] * product[i])
    return trace, cross


def values_of(trace, cross):
    lane = iota((trace.shape[0], 128), 1)
    terms = 2.0 * (trace * trace) - 2.0 * cross
    energy = jnp.sum(terms, axis=1, keepdims=True)
    tail = jnp.where(lane == 0, 1.0, jnp.where(lane == 1, energy, 0.0))
    return jnp.concatenate([trace, tail], axis=1)


def first_kernel(own_ref, other_ref, pair_ref, *refs):
    vector_refs, (out_ref, kept) = refs[:-2], refs[-2:]
    blocks = [own_ref[...], other_ref[...], pair_ref[0], pair_ref[1]]
    out_ref[...] = values_of(*sums_of(blocks, vector_refs, kept))


def second_kernel(log_ref, early_ref, own_ref, other_ref, near_ref, far_ref, back_ref, *refs):
    vector_refs, (out_ref, kept) = refs[:-2], refs[-2:]
    groups = 8
    blocks = [far_ref[0], far_ref[1], back_ref[0], back_ref[1]]
    late = values_of(*sums_of(blocks, vector_refs, kept))
    early = early_ref[...]
    width = early.shape[1]
    row = iota((groups, width), 0)
    lane = iota((groups, width), 1)
    for r in range(2):
        here = (row == 4 * r) & (lane == width - 126)
        early = jnp.where(here, log_ref[:, r : r + 1], early)
    me = lax.axis_index("chol")
    z, y = me // 2, me % 2
    values = [early, late]
    blocks = [[own_ref[...], other_ref[...], near_ref[0], near_ref[1]], blocks]
    rows = blocks[0][0].shape[0] - 8
    short = iota((groups, 128), 0)
    for h in range(2):
        tags = jnp.zeros((groups, 128), F32)
        for q in range(4):
            tags = jnp.where(short % 4 == q, blocks[h][q][rows:, :128].astype(F32), tags)
        wanted = [
            jnp.where(iota((groups, 1), 0) < 4, tags[:, k : k + 1], tags[:, 2 + k : 3 + k]) for k in range(2)
        ]
        owners = [((z + 2 * h + q // 2) % 4) * 2 + (y + q) % 2 for q in range(4)]
        for d in range(out_ref.shape[0] // groups):
            hit = (wanted[0] == float(d)) | (wanted[1] == float(d))
            packet = jnp.where(hit, values[h], 0.0)
            packet = packet[:4] + packet[4:]
            for q in range(4):
                out_ref[d * groups + owners[q]] = packet[q : q + 1, :]


def stops(kernel, shape, operands, vectors):
    elec = sum(part.shape[0] for part in vectors)
    _, count, basis = vectors[0].shape
    walkers = 8
    whole = pl.BlockSpec(memory_space=pltpu.VMEM)
    return pl.pallas_call(
        kernel,
        out_shape=jax.ShapeDtypeStruct(shape, F32),
        in_specs=[whole] * (len(operands) + len(vectors)),
        out_specs=whole,
        scratch_shapes=[pltpu.VMEM((elec, elec, walkers, count), F32)],
        cost_estimate=pl.CostEstimate(
            flops=2 * walkers * elec * elec * count * basis,
            bytes_accessed=2 * elec * count * basis,
            transcendentals=0,
        ),
        compiler_params=pltpu.CompilerParams(vmem_limit_bytes=16 * MIB),
    )(*operands, *vectors)


def slot_kernel(scale, packets_ref, energy_ref, bias_ref, log_ref):
    slots, total = bias_ref.shape
    groups = 8
    width = packets_ref.shape[2]
    count = total // groups
    filled = jnp.zeros((groups, 1), F32)
    held = [jnp.zeros((groups, width), F32) for _ in range(slots)]
    for s in range(packets_ref.shape[0] // groups):
        packet = jnp.concatenate([packets_ref[s * groups + c] for c in range(groups)], axis=0)
        flag = packet[:, count : count + 1]
        for t in range(slots):
            held[t] = jnp.where((flag > 0.5) & (filled == float(t)), packet, held[t])
        filled = filled + flag
    for t in range(slots):
        for c in range(groups):
            bias_ref[t : t + 1, c * count : (c + 1) * count] = held[t][c : c + 1, :count]
        energy_ref[t] = jnp.sum(held[t][:, count + 1 : count + 2]) * scale
        log_ref[t] = jnp.sum(held[t][:, count + 2 : count + 3])


def slots_of(packets, slots, total, scale):
    return pl.pallas_call(
        functools.partial(slot_kernel, scale),
        out_shape=(
            jax.ShapeDtypeStruct((slots,), F32),
            jax.ShapeDtypeStruct((slots, total), F32),
            jax.ShapeDtypeStruct((slots,), F32),
        ),
        in_specs=[pl.BlockSpec(memory_space=pltpu.VMEM)],
        out_specs=(
            pl.BlockSpec(memory_space=pltpu.SMEM),
            pl.BlockSpec(memory_space=pltpu.VMEM),
            pl.BlockSpec(memory_space=pltpu.SMEM),
        ),
        compiler_params=pltpu.CompilerParams(vmem_limit_bytes=4 * MIB),
        name="slots",
    )(packets)


def pair_kernel(first_ref, second_ref, out_ref):
    out_ref[0] = first_ref[...]
    out_ref[1] = second_ref[...]


def paired(first, second):
    return pl.pallas_call(
        pair_kernel,
        out_shape=jax.ShapeDtypeStruct((2,) + first.shape, first.dtype),
        in_specs=[pl.BlockSpec(memory_space=pltpu.VMEM)] * 2,
        out_specs=pl.BlockSpec(memory_space=pltpu.VMEM),
        compiler_params=pltpu.CompilerParams(vmem_limit_bytes=MIB),
        name="pair",
    )(first, second)


def moved(value, dz, dy):
    pairs = [
        (z * 2 + y, ((z + dz) % 4) * 2 + (y + dy) % 2) for z in range(4) for y in range(2)
    ]
    return lax.ppermute(value, "chol", pairs)


def body(orbitals, dest, chol_vectors):
    walk_count, chol_count = lax.axis_size("walk"), lax.axis_size("chol")
    walk_dev, elec, _ = orbitals.shape
    local = chol_vectors.shape[0]
    total = chol_count * local
    width = local + 128
    dest = pltpu.with_memory_space_constraint(dest, pltpu.HBM)
    orbitals = pltpu.with_memory_space_constraint(orbitals, pltpu.HBM)
    chol_vectors = pltpu.with_memory_space_constraint(chol_vectors, pltpu.HBM)
    packet, log = green_of(dest, orbitals)
    other = moved(packet, 0, 1)
    pair = paired(packet, other)
    near = moved(pair, -1, 0)
    far = moved(pair, 2, 0)
    back = moved(pair, 1, 0)
    lower = relayout(chol_vectors, 0, elec // 2)
    upper = relayout(chol_vectors, elec // 2, elec // 2)
    vectors = [lower, upper]
    early = stops(first_kernel, (8, width), [packet, other, near], vectors)
    packets = stops(
        second_kernel,
        (walk_count * chol_count, 1, width),
        [log, early, packet, other, near, far, back],
        vectors,
    )
    packets = lax.all_to_all(packets, ("walk", "chol"), split_axis=0, concat_axis=0, tiled=True)
    return slots_of(packets, 2 * walk_dev, total, 1.0 / (elec * total))


def solution(mesh):
    placed = (P(("walk", "chol"), None, None), P(("walk", "chol"), None), P("chol", None, None))
    return jax.shard_map(
        body,
        mesh=mesh,
        in_specs=placed,
        out_specs=(P(("walk", "chol")), P(("walk", "chol"), None), P(("walk", "chol"))),
        check_vma=False,
    )
```

```python
import functools

import jax
import jax.numpy as jnp
from jax import lax
from jax.experimental import pallas as pl
from jax.experimental.pallas import tpu as pltpu
from jax.sharding import PartitionSpec as P

F32 = jnp.float32
BF16 = jnp.bfloat16
MIB = 1 << 20
HIGH = lax.Precision.HIGHEST


def iota(shape, axis):
    return lax.broadcasted_iota(jnp.int32, shape, axis)


def normal_rows(walkers):
    elec, basis = walkers.shape
    whole = lax.dot_general(
        walkers[:, :elec], walkers, (((0,), (0,)), ((), ())), precision=HIGH, preferred_element_type=F32
    )
    return [[whole[n : n + 8, t : t + 128] for t in range(0, basis, 128)] for n in range(0, elec, 8)]


def eliminate(parts, pivots, k):
    home, at = k // 8, k % 8
    sub = iota((8, 128), 0)
    lane = iota((1, 128), 1)
    upper = [tile[at : at + 1] for tile in parts[home]]
    lower = [tile[at + 1 : at + 2] for tile in parts[home]]

    def spread(tile, n):
        return jnp.broadcast_to(tile[:, n : n + 1], tile.shape)

    left = [spread(part[0], k) for part in parts]
    right = [spread(part[0], k + 1) for part in parts]
    pivot, below = spread(upper[0], k), spread(lower[0], k)
    inverse = 1.0 / pivot
    link = spread(upper[0], k + 1) * inverse
    after = spread(lower[0], k + 1) - below * link
    inverse_after = 1.0 / after
    tops = [tile * inverse for tile in upper]
    bottoms = [(tile - below * top) * inverse_after for tile, top in zip(lower, tops)]
    uppers = [top - link * bottom for top, bottom in zip(tops, bottoms)]
    right = [b - a * link for a, b in zip(left, right)]
    pivots = jnp.where(lane == k, pivot, jnp.where(lane == k + 1, after, pivots))
    out = []
    for n, part in enumerate(parts):
        tiles = []
        for tile, top, bottom, first in zip(part, tops, bottoms, uppers):
            new = (tile - left[n] * top) - right[n] * bottom
            if n == home:
                new = jnp.where(sub == at, first, jnp.where(sub == at + 1, bottom, new))
            tiles.append(new)
        out.append(tiles)
    return out, pivots


def green_kernel(
    places_ref, orbitals_ref, vectors_ref, packet_ref, log_ref, raw_ref, dest_ref, walkers, landed, arrived
):
    count, elec, _ = walkers.shape
    fetch = pltpu.make_async_copy(orbitals_ref, walkers, landed.at[0])
    fetch.start()
    read = pltpu.make_async_copy(places_ref, dest_ref, landed.at[1])
    read.start()
    ahead = pltpu.make_async_copy(vectors_ref.at[:, pl.ds(0, raw_ref.shape[1]), :], raw_ref, arrived)
    ahead.start()
    fetch.wait()
    read.wait()
    pivots = [jnp.ones((1, 128), F32) for _ in range(count)]
    parts = [normal_rows(walkers[r]) for r in range(count)]
    for k in range(0, elec, 2):
        for r in range(count):
            parts[r], pivots[r] = eliminate(parts[r], pivots[r], k)
    out = jnp.zeros((8, 128), F32)
    lane = iota((1, 128), 1)
    lanes = iota((8, 128), 1)
    for r in range(count):
        wanted = (dest_ref[r, 0] >= 0) | (dest_ref[r, 1] >= 0)
        green = jnp.where(wanted, jnp.concatenate([jnp.concatenate(part, axis=1) for part in parts[r]], axis=0), 0.0)
        tag = jnp.where(
            lane == 0, dest_ref[r, 0].astype(F32), jnp.where(lane == 1, dest_ref[r, 1].astype(F32), 0.0)
        )
        rows = slice(r * elec, (r + 1) * elec)
        packet_ref[rows, :128] = jnp.where(lane < elec, tag, green[:, :128]).astype(BF16)
        packet_ref[rows, 128:] = green[:, 128:].astype(BF16)
        log = jnp.sum(jnp.where(lane < elec, jnp.log(pivots[r]), 0.0), axis=1, keepdims=True)
        log = jnp.where(wanted, log * (0.5 / elec), 0.0)
        out = jnp.where(lanes == r, log, out)
    log_ref[...] = out
    ahead.wait()


def green_of(dest, orbitals, vectors):
    count, elec, basis = orbitals.shape
    hbm = pl.BlockSpec(memory_space=pltpu.HBM)
    vmem = pl.BlockSpec(memory_space=pltpu.VMEM)
    return pl.pallas_call(
        green_kernel,
        out_shape=(
            jax.ShapeDtypeStruct((count * elec, basis), BF16),
            jax.ShapeDtypeStruct((8, 128), F32),
            jax.ShapeDtypeStruct((vectors.shape[0], elec // 2, basis), BF16),
        ),
        in_specs=[hbm, hbm, hbm],
        out_specs=(vmem, vmem, vmem),
        scratch_shapes=[
            pltpu.SMEM(dest.shape, jnp.int32),
            pltpu.VMEM(orbitals.shape, F32),
            pltpu.SemaphoreType.DMA((2,)),
            pltpu.SemaphoreType.DMA,
        ],
        cost_estimate=pl.CostEstimate(flops=8_000_000, bytes_accessed=4_400_000, transcendentals=64),
        compiler_params=pltpu.CompilerParams(vmem_limit_bytes=4 * MIB),
        name="green",
    )(dest, orbitals, vectors)


def relayout_kernel(raw_ref, vectors_ref, out_ref, held, arrived):
    count, half, basis = held.shape
    chunks = arrived.shape[0]
    size = count // chunks
    group = 16

    def copy(n):
        part = pl.ds(n * size, size)
        return pltpu.make_async_copy(
            vectors_ref.at[part, pl.ds(half, half), :], held.at[part], arrived.at[n]
        )

    for n in range(chunks):
        copy(n).start()
    rows = group * half
    to = iota((rows, rows), 0)
    of = iota((rows, rows), 1)
    move = ((to % group) * half + to // group == of).astype(BF16)
    for h, ref in enumerate((raw_ref, held)):
        for n in range(chunks):
            if h:
                copy(n).wait()
            for b in range(n * size // group, (n + 1) * size // group):
                part = slice(b * group, (b + 1) * group)
                moved = jnp.dot(move, ref[part].reshape(rows, basis), preferred_element_type=F32)
                out_ref[h * half : (h + 1) * half, part, :] = moved.reshape(half, group, basis).astype(BF16)


def relayout(raw, vectors):
    count, elec, basis = vectors.shape
    chunks = 4
    vmem = pl.BlockSpec(memory_space=pltpu.VMEM)
    return pl.pallas_call(
        relayout_kernel,
        out_shape=jax.ShapeDtypeStruct((elec, count, basis), BF16),
        in_specs=[vmem, pl.BlockSpec(memory_space=pltpu.HBM)],
        out_specs=vmem,
        scratch_shapes=[pltpu.VMEM(raw.shape, BF16), pltpu.SemaphoreType.DMA((chunks,))],
        cost_estimate=pl.CostEstimate(
            flops=2 * count * elec * basis * 256, bytes_accessed=2 * count * elec * basis, transcendentals=0
        ),
        compiler_params=pltpu.CompilerParams(vmem_limit_bytes=10 * MIB),
        name="relayout",
    )(raw, vectors)


def sums_of(blocks, vector_refs, kept):
    elec, _, walkers, count = kept.shape
    per = walkers // len(blocks)
    size = walkers * elec
    stacked = jnp.concatenate(blocks, axis=0)
    to = iota((size, size), 0)
    of = iota((size, size), 1)
    j, r, q = to // walkers, (to // len(blocks)) % per, to % len(blocks)
    move = ((q * per + r) * elec + j == of).astype(BF16)
    green = jnp.dot(move, stacked, preferred_element_type=F32)
    row, lane = iota((size, 128), 0), iota((size, 128), 1)
    head = jnp.where(lane < elec, (lane == row // walkers).astype(F32), green[:, :128])
    green = jnp.concatenate([head, green[:, 128:]], axis=1).astype(BF16)
    trace = jnp.zeros((walkers, count), F32)
    cross = jnp.zeros((walkers, count), F32)
    for i in range(elec):
        ref = vector_refs[i * len(vector_refs) // elec]
        product = lax.dot_general(
            green, ref[i % ref.shape[0]], (((1,), (1,)), ((), ())), preferred_element_type=F32
        ).reshape(elec, walkers, count)
        for j in range(i + 1, elec):
            kept[j, i] = product[j]
        for j in range(i):
            cross = cross + product[j] * kept[i, j]
        trace = trace + product[i]
        cross = cross + 0.5 * (product[i] * product[i])
    return trace, cross


def values_of(trace, cross):
    lane = iota((trace.shape[0], 128), 1)
    terms = 2.0 * (trace * trace) - 2.0 * cross
    energy = jnp.sum(terms, axis=1, keepdims=True)
    tail = jnp.where(lane == 0, 1.0, jnp.where(lane == 1, energy, 0.0))
    return jnp.concatenate([trace, tail], axis=1)


def first_kernel(own_ref, other_ref, pair_ref, *refs):
    vector_refs, (out_ref, kept) = refs[:-2], refs[-2:]
    blocks = [own_ref[...], other_ref[...], pair_ref[0], pair_ref[1]]
    out_ref[...] = values_of(*sums_of(blocks, vector_refs, kept))


def second_kernel(log_ref, early_ref, own_ref, other_ref, near_ref, far_ref, back_ref, *refs):
    vector_refs, (out_ref, kept) = refs[:-2], refs[-2:]
    groups = 8
    blocks = [far_ref[0], far_ref[1], back_ref[0], back_ref[1]]
    late = values_of(*sums_of(blocks, vector_refs, kept))
    early = early_ref[...]
    width = early.shape[1]
    row = iota((groups, width), 0)
    lane = iota((groups, width), 1)
    for r in range(2):
        here = (row == 4 * r) & (lane == width - 126)
        early = jnp.where(here, log_ref[:, r : r + 1], early)
    me = lax.axis_index("chol")
    z, y = me // 2, me % 2
    values = [early, late]
    blocks = [[own_ref[...], other_ref[...], near_ref[0], near_ref[1]], blocks]
    rows = blocks[0][0].shape[0] // 2
    short = iota((groups, 128), 0)
    for h in range(2):
        tags = jnp.zeros((groups, 128), F32)
        for r in range(2):
            for q in range(4):
                tag = blocks[h][q][r * rows : r * rows + 16, :128].astype(F32)[:groups]
                tags = jnp.where(short == 4 * r + q, tag, tags)
        wanted = [tags[:, k : k + 1] for k in range(2)]
        owners = [((z + 2 * h + q // 2) % 4) * 2 + (y + q) % 2 for q in range(4)]
        for d in range(out_ref.shape[0] // groups):
            hit = (wanted[0] == float(d)) | (wanted[1] == float(d))
            packet = jnp.where(hit, values[h], 0.0)
            packet = packet[:4] + packet[4:]
            for q in range(4):
                out_ref[d * groups + owners[q]] = packet[q : q + 1, :]


def stops(kernel, shape, operands, vectors):
    elec = sum(part.shape[0] for part in vectors)
    _, count, basis = vectors[0].shape
    walkers = 8
    whole = pl.BlockSpec(memory_space=pltpu.VMEM)
    return pl.pallas_call(
        kernel,
        out_shape=jax.ShapeDtypeStruct(shape, F32),
        in_specs=[whole] * (len(operands) + len(vectors)),
        out_specs=whole,
        scratch_shapes=[pltpu.VMEM((elec, elec, walkers, count), F32)],
        cost_estimate=pl.CostEstimate(
            flops=2 * walkers * elec * elec * count * basis,
            bytes_accessed=2 * elec * count * basis,
            transcendentals=0,
        ),
        compiler_params=pltpu.CompilerParams(vmem_limit_bytes=16 * MIB),
    )(*operands, *vectors)


def slot_kernel(scale, packets_ref, energy_ref, bias_ref, log_ref):
    slots, total = bias_ref.shape
    groups = 8
    width = packets_ref.shape[2]
    count = total // groups
    filled = jnp.zeros((groups, 1), F32)
    held = [jnp.zeros((groups, width), F32) for _ in range(slots)]
    for s in range(packets_ref.shape[0] // groups):
        packet = jnp.concatenate([packets_ref[s * groups + c] for c in range(groups)], axis=0)
        flag = packet[:, count : count + 1]
        for t in range(slots):
            held[t] = jnp.where((flag > 0.5) & (filled == float(t)), packet, held[t])
        filled = filled + flag
    for t in range(slots):
        for c in range(groups):
            bias_ref[t : t + 1, c * count : (c + 1) * count] = held[t][c : c + 1, :count]
        energy_ref[t] = jnp.sum(held[t][:, count + 1 : count + 2]) * scale
        log_ref[t] = jnp.sum(held[t][:, count + 2 : count + 3])


def slots_of(packets, slots, total, scale):
    return pl.pallas_call(
        functools.partial(slot_kernel, scale),
        out_shape=(
            jax.ShapeDtypeStruct((slots,), F32),
            jax.ShapeDtypeStruct((slots, total), F32),
            jax.ShapeDtypeStruct((slots,), F32),
        ),
        in_specs=[pl.BlockSpec(memory_space=pltpu.VMEM)],
        out_specs=(
            pl.BlockSpec(memory_space=pltpu.SMEM),
            pl.BlockSpec(memory_space=pltpu.VMEM),
            pl.BlockSpec(memory_space=pltpu.SMEM),
        ),
        compiler_params=pltpu.CompilerParams(vmem_limit_bytes=4 * MIB),
        name="slots",
    )(packets)


def pair_kernel(first_ref, second_ref, out_ref):
    out_ref[0] = first_ref[...]
    out_ref[1] = second_ref[...]


def paired(first, second):
    return pl.pallas_call(
        pair_kernel,
        out_shape=jax.ShapeDtypeStruct((2,) + first.shape, first.dtype),
        in_specs=[pl.BlockSpec(memory_space=pltpu.VMEM)] * 2,
        out_specs=pl.BlockSpec(memory_space=pltpu.VMEM),
        compiler_params=pltpu.CompilerParams(vmem_limit_bytes=MIB),
        name="pair",
    )(first, second)


def moved(value, dz, dy):
    pairs = [
        (z * 2 + y, ((z + dz) % 4) * 2 + (y + dy) % 2) for z in range(4) for y in range(2)
    ]
    return lax.ppermute(value, "chol", pairs)


def body(orbitals, dest, chol_vectors):
    walk_count, chol_count = lax.axis_size("walk"), lax.axis_size("chol")
    walk_dev, elec, _ = orbitals.shape
    local = chol_vectors.shape[0]
    total = chol_count * local
    width = local + 128
    dest = pltpu.with_memory_space_constraint(dest, pltpu.HBM)
    orbitals = pltpu.with_memory_space_constraint(orbitals, pltpu.HBM)
    chol_vectors = pltpu.with_memory_space_constraint(chol_vectors, pltpu.HBM)
    packet, log, raw = green_of(dest, orbitals, chol_vectors)
    other = moved(packet, 0, 1)
    pair = paired(packet, other)
    near = moved(pair, -1, 0)
    far = moved(pair, 2, 0)
    back = moved(pair, 1, 0)
    vectors = [relayout(raw, chol_vectors)]
    early = stops(first_kernel, (8, width), [packet, other, near], vectors)
    packets = stops(
        second_kernel, (walk_count * chol_count, 1, width), [log, early, packet, other, near, far, back], vectors
    )
    packets = lax.all_to_all(packets, ("walk", "chol"), split_axis=0, concat_axis=0, tiled=True)
    return slots_of(packets, 2 * walk_dev, total, 1.0 / (elec * total))


def solution(mesh):
    placed = (P(("walk", "chol"), None, None), P(("walk", "chol"), None), P("chol", None, None))
    return jax.shard_map(
        body,
        mesh=mesh,
        in_specs=placed,
        out_specs=(P(("walk", "chol")), P(("walk", "chol"), None), P(("walk", "chol"))),
        check_vma=False,
    )
```

```python
import functools

import jax
import jax.numpy as jnp
from jax import lax
from jax.experimental import pallas as pl
from jax.experimental.pallas import tpu as pltpu
from jax.sharding import PartitionSpec as P

F32 = jnp.float32
BF16 = jnp.bfloat16
MIB = 1 << 20
HIGH = lax.Precision.HIGHEST


def iota(shape, axis):
    return lax.broadcasted_iota(jnp.int32, shape, axis)


def normal_rows(walkers):
    elec, basis = walkers.shape
    whole = lax.dot_general(
        walkers[:, :elec], walkers, (((0,), (0,)), ((), ())), precision=HIGH, preferred_element_type=F32
    )
    return [[whole[n : n + 8, t : t + 128] for t in range(0, basis, 128)] for n in range(0, elec, 8)]


def eliminate(parts, pivots, k, step):
    home, at = k // 8, k % 8
    sub = iota((8, 128), 0)
    lane = iota((1, 128), 1)

    def spread(tile, n):
        return jnp.broadcast_to(tile[:, n : n + 1], tile.shape)

    columns = [[spread(part[0], k + c) for part in parts] for c in range(step)]
    rows = [[tile[at + c : at + c + 1] for tile in parts[home]] for c in range(step)]
    corner = [[spread(row[0], k + c) for c in range(step)] for row in rows]
    tops = []
    for c in range(step):
        pivots = jnp.where(lane == k + c, corner[c][c], pivots)
        inverse = 1.0 / corner[c][c]
        corner[c] = [value * inverse for value in corner[c]]
        rows[c] = [tile * inverse for tile in rows[c]]
        tops.append(rows[c])
        for e in range(c + 1, step):
            columns[e] = [x - y * corner[c][e] for x, y in zip(columns[e], columns[c])]
        for o in range(step):
            if o != c:
                factor = corner[o][c]
                corner[o] = [x - factor * y if e > c else x for e, (x, y) in enumerate(zip(corner[o], corner[c]))]
                rows[o] = [x - factor * y for x, y in zip(rows[o], rows[c])]
    out = []
    for n, part in enumerate(parts):
        tiles = []
        for t, tile in enumerate(part):
            for c in range(step):
                tile = tile - columns[c][n] * tops[c][t]
            if n == home:
                for c in range(step):
                    tile = jnp.where(sub == at + c, rows[c][t], tile)
            tiles.append(tile)
        out.append(tiles)
    return out, pivots


def green_kernel(
    places_ref, orbitals_ref, vectors_ref, packet_ref, log_ref, raw_ref, dest_ref, walkers, landed, arrived
):
    count, elec, _ = walkers.shape
    fetch = pltpu.make_async_copy(orbitals_ref, walkers, landed.at[0])
    fetch.start()
    read = pltpu.make_async_copy(places_ref, dest_ref, landed.at[1])
    read.start()
    ahead = pltpu.make_async_copy(vectors_ref.at[:, pl.ds(0, raw_ref.shape[1]), :], raw_ref, arrived)
    ahead.start()
    fetch.wait()
    read.wait()
    pivots = [jnp.ones((1, 128), F32) for _ in range(count)]
    parts = [normal_rows(walkers[r]) for r in range(count)]
    step = 4
    for k in range(0, elec, step):
        for r in range(count):
            parts[r], pivots[r] = eliminate(parts[r], pivots[r], k, step)
    out = jnp.zeros((8, 128), F32)
    lane = iota((1, 128), 1)
    lanes = iota((8, 128), 1)
    for r in range(count):
        wanted = (dest_ref[r, 0] >= 0) | (dest_ref[r, 1] >= 0)
        green = jnp.where(wanted, jnp.concatenate([jnp.concatenate(part, axis=1) for part in parts[r]], axis=0), 0.0)
        tag = jnp.where(
            lane == 0, dest_ref[r, 0].astype(F32), jnp.where(lane == 1, dest_ref[r, 1].astype(F32), 0.0)
        )
        rows = slice(r * elec, (r + 1) * elec)
        packet_ref[rows, :128] = jnp.where(lane < elec, tag, green[:, :128]).astype(BF16)
        packet_ref[rows, 128:] = green[:, 128:].astype(BF16)
        log = jnp.sum(jnp.where(lane < elec, jnp.log(pivots[r]), 0.0), axis=1, keepdims=True)
        log = jnp.where(wanted, log * (0.5 / elec), 0.0)
        out = jnp.where(lanes == r, log, out)
    log_ref[...] = out
    ahead.wait()


def green_of(dest, orbitals, vectors):
    count, elec, basis = orbitals.shape
    hbm = pl.BlockSpec(memory_space=pltpu.HBM)
    vmem = pl.BlockSpec(memory_space=pltpu.VMEM)
    return pl.pallas_call(
        green_kernel,
        out_shape=(
            jax.ShapeDtypeStruct((count * elec, basis), BF16),
            jax.ShapeDtypeStruct((8, 128), F32),
            jax.ShapeDtypeStruct((vectors.shape[0], elec // 2, basis), BF16),
        ),
        in_specs=[hbm, hbm, hbm],
        out_specs=(vmem, vmem, vmem),
        scratch_shapes=[
            pltpu.SMEM(dest.shape, jnp.int32),
            pltpu.VMEM(orbitals.shape, F32),
            pltpu.SemaphoreType.DMA((2,)),
            pltpu.SemaphoreType.DMA,
        ],
        cost_estimate=pl.CostEstimate(flops=8_000_000, bytes_accessed=4_400_000, transcendentals=64),
        compiler_params=pltpu.CompilerParams(vmem_limit_bytes=4 * MIB),
        name="green",
    )(dest, orbitals, vectors)


def relayout_kernel(raw_ref, vectors_ref, out_ref, held, arrived):
    count, half, basis = held.shape
    chunks = arrived.shape[0]
    size = count // chunks
    group = 16

    def copy(n):
        part = pl.ds(n * size, size)
        return pltpu.make_async_copy(
            vectors_ref.at[part, pl.ds(half, half), :], held.at[part], arrived.at[n]
        )

    for n in range(chunks):
        copy(n).start()
    rows = group * half
    to = iota((rows, rows), 0)
    of = iota((rows, rows), 1)
    move = ((to % group) * half + to // group == of).astype(BF16)
    for h, ref in enumerate((raw_ref, held)):
        for n in range(chunks):
            if h:
                copy(n).wait()
            for b in range(n * size // group, (n + 1) * size // group):
                part = slice(b * group, (b + 1) * group)
                moved = jnp.dot(move, ref[part].reshape(rows, basis), preferred_element_type=F32)
                out_ref[h * half : (h + 1) * half, part, :] = moved.reshape(half, group, basis).astype(BF16)


def relayout(raw, vectors):
    count, elec, basis = vectors.shape
    chunks = 4
    vmem = pl.BlockSpec(memory_space=pltpu.VMEM)
    return pl.pallas_call(
        relayout_kernel,
        out_shape=jax.ShapeDtypeStruct((elec, count, basis), BF16),
        in_specs=[vmem, pl.BlockSpec(memory_space=pltpu.HBM)],
        out_specs=vmem,
        scratch_shapes=[pltpu.VMEM(raw.shape, BF16), pltpu.SemaphoreType.DMA((chunks,))],
        cost_estimate=pl.CostEstimate(
            flops=2 * count * elec * basis * 256, bytes_accessed=2 * count * elec * basis, transcendentals=0
        ),
        compiler_params=pltpu.CompilerParams(vmem_limit_bytes=10 * MIB),
        name="relayout",
    )(raw, vectors)


def sums_of(blocks, vector_refs, kept):
    elec, _, walkers, count = kept.shape
    per = walkers // len(blocks)
    size = walkers * elec
    stacked = jnp.concatenate(blocks, axis=0)
    to = iota((size, size), 0)
    of = iota((size, size), 1)
    j, r, q = to // walkers, (to // len(blocks)) % per, to % len(blocks)
    move = ((q * per + r) * elec + j == of).astype(BF16)
    green = jnp.dot(move, stacked, preferred_element_type=F32)
    row, lane = iota((size, 128), 0), iota((size, 128), 1)
    head = jnp.where(lane < elec, (lane == row // walkers).astype(F32), green[:, :128])
    green = jnp.concatenate([head, green[:, 128:]], axis=1).astype(BF16)
    trace = jnp.zeros((walkers, count), F32)
    cross = jnp.zeros((walkers, count), F32)
    for i in range(elec):
        ref = vector_refs[i * len(vector_refs) // elec]
        product = lax.dot_general(
            green, ref[i % ref.shape[0]], (((1,), (1,)), ((), ())), preferred_element_type=F32
        ).reshape(elec, walkers, count)
        for j in range(i + 1, elec):
            kept[j, i] = product[j]
        for j in range(i):
            cross = cross + product[j] * kept[i, j]
        trace = trace + product[i]
        cross = cross + 0.5 * (product[i] * product[i])
    return trace, cross


def values_of(trace, cross):
    lane = iota((trace.shape[0], 128), 1)
    terms = 2.0 * (trace * trace) - 2.0 * cross
    energy = jnp.sum(terms, axis=1, keepdims=True)
    tail = jnp.where(lane == 0, 1.0, jnp.where(lane == 1, energy, 0.0))
    return jnp.concatenate([trace, tail], axis=1)


def first_kernel(own_ref, other_ref, pair_ref, *refs):
    vector_refs, (out_ref, kept) = refs[:-2], refs[-2:]
    blocks = [own_ref[...], other_ref[...], pair_ref[0], pair_ref[1]]
    out_ref[...] = values_of(*sums_of(blocks, vector_refs, kept))


def second_kernel(log_ref, early_ref, own_ref, other_ref, near_ref, far_ref, across_ref, back_ref, *refs):
    vector_refs, (out_ref, kept) = refs[:-2], refs[-2:]
    groups = 8
    blocks = [far_ref[...], across_ref[...], back_ref[0], back_ref[1]]
    late = values_of(*sums_of(blocks, vector_refs, kept))
    early = early_ref[...]
    width = early.shape[1]
    row = iota((groups, width), 0)
    lane = iota((groups, width), 1)
    for r in range(2):
        here = (row == 4 * r) & (lane == width - 126)
        early = jnp.where(here, log_ref[:, r : r + 1], early)
    me = lax.axis_index("chol")
    z, y = me // 2, me % 2
    values = [early, late]
    blocks = [[own_ref[...], other_ref[...], near_ref[0], near_ref[1]], blocks]
    rows = blocks[0][0].shape[0] // 2
    short = iota((groups, 128), 0)
    for h in range(2):
        tags = jnp.zeros((groups, 128), F32)
        for r in range(2):
            for q in range(4):
                tag = blocks[h][q][r * rows : r * rows + 16, :128].astype(F32)[:groups]
                tags = jnp.where(short == 4 * r + q, tag, tags)
        wanted = [tags[:, k : k + 1] for k in range(2)]
        owners = [((z + 2 * h + q // 2) % 4) * 2 + (y + q) % 2 for q in range(4)]
        for d in range(out_ref.shape[0] // groups):
            hit = (wanted[0] == float(d)) | (wanted[1] == float(d))
            packet = jnp.where(hit, values[h], 0.0)
            packet = packet[:4] + packet[4:]
            for q in range(4):
                out_ref[d * groups + owners[q]] = packet[q : q + 1, :]


def stops(kernel, shape, operands, vectors):
    elec = sum(part.shape[0] for part in vectors)
    _, count, basis = vectors[0].shape
    walkers = 8
    whole = pl.BlockSpec(memory_space=pltpu.VMEM)
    return pl.pallas_call(
        kernel,
        out_shape=jax.ShapeDtypeStruct(shape, F32),
        in_specs=[whole] * (len(operands) + len(vectors)),
        out_specs=whole,
        scratch_shapes=[pltpu.VMEM((elec, elec, walkers, count), F32)],
        cost_estimate=pl.CostEstimate(
            flops=2 * walkers * elec * elec * count * basis,
            bytes_accessed=2 * elec * count * basis,
            transcendentals=0,
        ),
        compiler_params=pltpu.CompilerParams(vmem_limit_bytes=16 * MIB),
    )(*operands, *vectors)


def slot_kernel(scale, packets_ref, energy_ref, bias_ref, log_ref):
    slots, total = bias_ref.shape
    groups = 8
    width = packets_ref.shape[2]
    count = total // groups
    filled = jnp.zeros((groups, 1), F32)
    held = [jnp.zeros((groups, width), F32) for _ in range(slots)]
    for s in range(packets_ref.shape[0] // groups):
        packet = jnp.concatenate([packets_ref[s * groups + c] for c in range(groups)], axis=0)
        flag = packet[:, count : count + 1]
        for t in range(slots):
            held[t] = jnp.where((flag > 0.5) & (filled == float(t)), packet, held[t])
        filled = filled + flag
    for t in range(slots):
        for c in range(groups):
            bias_ref[t : t + 1, c * count : (c + 1) * count] = held[t][c : c + 1, :count]
        energy_ref[t] = jnp.sum(held[t][:, count + 1 : count + 2]) * scale
        log_ref[t] = jnp.sum(held[t][:, count + 2 : count + 3])


def slots_of(packets, slots, total, scale):
    return pl.pallas_call(
        functools.partial(slot_kernel, scale),
        out_shape=(
            jax.ShapeDtypeStruct((slots,), F32),
            jax.ShapeDtypeStruct((slots, total), F32),
            jax.ShapeDtypeStruct((slots,), F32),
        ),
        in_specs=[pl.BlockSpec(memory_space=pltpu.VMEM)],
        out_specs=(
            pl.BlockSpec(memory_space=pltpu.SMEM),
            pl.BlockSpec(memory_space=pltpu.VMEM),
            pl.BlockSpec(memory_space=pltpu.SMEM),
        ),
        compiler_params=pltpu.CompilerParams(vmem_limit_bytes=4 * MIB),
        name="slots",
    )(packets)


def pair_kernel(first_ref, second_ref, out_ref):
    out_ref[0] = first_ref[...]
    out_ref[1] = second_ref[...]


def paired(first, second):
    return pl.pallas_call(
        pair_kernel,
        out_shape=jax.ShapeDtypeStruct((2,) + first.shape, first.dtype),
        in_specs=[pl.BlockSpec(memory_space=pltpu.VMEM)] * 2,
        out_specs=pl.BlockSpec(memory_space=pltpu.VMEM),
        compiler_params=pltpu.CompilerParams(vmem_limit_bytes=MIB),
        name="pair",
    )(first, second)


def moved(value, dz, dy):
    pairs = [
        (z * 2 + y, ((z + dz) % 4) * 2 + (y + dy) % 2) for z in range(4) for y in range(2)
    ]
    return lax.ppermute(value, "chol", pairs)


def body(orbitals, dest, chol_vectors):
    walk_count, chol_count = lax.axis_size("walk"), lax.axis_size("chol")
    walk_dev, elec, _ = orbitals.shape
    local = chol_vectors.shape[0]
    total = chol_count * local
    width = local + 128
    dest = pltpu.with_memory_space_constraint(dest, pltpu.HBM)
    orbitals = pltpu.with_memory_space_constraint(orbitals, pltpu.HBM)
    chol_vectors = pltpu.with_memory_space_constraint(chol_vectors, pltpu.HBM)
    packet, log, raw = green_of(dest, orbitals, chol_vectors)
    other = moved(packet, 0, 1)
    far = moved(packet, 2, 0)
    pair = paired(packet, other)
    near = moved(pair, -1, 0)
    across = moved(far, 0, 1)
    back = moved(pair, 1, 0)
    vectors = [relayout(raw, chol_vectors)]
    early = stops(first_kernel, (8, width), [packet, other, near], vectors)
    packets = stops(
        second_kernel,
        (walk_count * chol_count, 1, width),
        [log, early, packet, other, near, far, across, back],
        vectors,
    )
    packets = lax.all_to_all(packets, ("walk", "chol"), split_axis=0, concat_axis=0, tiled=True)
    return slots_of(packets, 2 * walk_dev, total, 1.0 / (elec * total))


def solution(mesh):
    placed = (P(("walk", "chol"), None, None), P(("walk", "chol"), None), P("chol", None, None))
    return jax.shard_map(
        body,
        mesh=mesh,
        in_specs=placed,
        out_specs=(P(("walk", "chol")), P(("walk", "chol"), None), P(("walk", "chol"))),
        check_vma=False,
    )
```
